32 devices in a mesh: fiber: 16 (over z, y, core), freq: 2 (over x).
Axes of the slice: x: 2, y: 2, z: 4, core: 2. Of those that a mesh axis runs over, the one named last changes fastest.
Arguments:
- spectra: bfloat16 [2, 512, 16, 2048], P(None, 'freq', 'fiber'), may hold values from -128 to 128
- valid_mask: int32 [16, 2048], P('fiber'), may hold values 0 or 1
- pair_reach: int32 [16], replicated, may hold values from 1 to 2, as said below
Outputs:
- correlations: float32 [16, 5, 2, 128, 128], P('fiber', None, 'freq')
The draws below stay inside these ranges and needn't reach their ends.
Inputs may be any that keep to these rules, and one draw needn't show every extreme that they name: Block b is paired with blocks b + 1 to b + pair_reach[b]; every draw holds some block with reach 1 and some with reach 2.
All inputs are finite; a program needn't handle non-finite values. No bound on the sum of `valid_mask` on one device may be relied on, other than what follows from the above.
Results may differ from the reference program's by a relative error of at most 0.0012.
Values may be sent and summed in bfloat16 or wider, within the bound.
A program may use at most 128 MiB of HBM per device.

```python
import jax
import jax.numpy as jnp
from jax import lax

BLOCK = 128
FREQS = 512
BAND = 2
WINDOWS = 16
NBLOCKS = 16
CHANNELS = 2048
LAGS = 2


def draw_spectra(key, part):
    bins = jnp.arange(FREQS, dtype=jnp.float32) / FREQS
    ramp = 1.0 + bins
    rough = jnp.exp(jax.random.uniform(jax.random.fold_in(key, 1), (FREQS,), jnp.float32, jnp.log(0.6), jnp.log(1.6)))
    scales = jnp.exp(jax.random.uniform(jax.random.fold_in(key, 2), (WINDOWS, CHANNELS), jnp.float32, 0.0, jnp.log(10.0)))
    noise = jnp.clip(jax.random.normal(jax.random.fold_in(key, 3), (2, FREQS, WINDOWS, CHANNELS), jnp.float32), -4.0, 4.0)
    result = noise * (ramp * rough)[None, :, None, None] * scales[None, None]
    return result.astype(jnp.bfloat16)


def draw_pair_reach(key, part):
    base = jax.random.randint(jax.random.fold_in(key, 11), (NBLOCKS,), 1, BAND + 1)
    order = jax.random.permutation(jax.random.fold_in(key, 12), NBLOCKS)
    base = base.at[order[0]].set(BAND)
    base = base.at[order[1]].set(1)
    return base.astype(jnp.int32)


def touch_ends(entries, own_key, least, top_value):
    index_at = [jax.random.randint(jax.random.fold_in(own_key, axis), (), 0, length) for axis, length in enumerate(entries.shape)]
    main_axis = entries.shape.index(max(entries.shape))
    next_to = index_at[:main_axis] + [(index_at[main_axis] + 1) % entries.shape[main_axis]] + index_at[main_axis + 1:]
    return entries.at[tuple(index_at)].set(least).at[tuple(next_to)].set(top_value)


def setup_inputs(seed: int = 0) -> dict:
    arg_keys = jax.random.split(jax.random.key(seed), 4)
    spectra = draw_spectra(jax.random.fold_in(arg_keys[3], 71), 0)
    valid_mask = touch_ends((jax.random.randint(arg_keys[1], (WINDOWS, CHANNELS), 0, 8) < 7).astype(jnp.int32), jax.random.fold_in(arg_keys[1], 1), 0, 1)
    pair_reach = draw_pair_reach(jax.random.fold_in(arg_keys[3], 71), 0)
    return {"spectra": spectra, "valid_mask": valid_mask, "pair_reach": pair_reach}


first_bin = 64.0
lag_step = 24.0
transform_length = 2048.0

def twiddles(bins, lag_count):
    lag_values = jnp.arange(lag_count, dtype=jnp.float32) * lag_step
    angle = 2.0 * jnp.pi / transform_length * lag_values[:, None] * (first_bin + bins)[None, :]
    return jnp.concatenate([jnp.cos(angle), -jnp.sin(angle)], axis=1)

def correlate(left_block, right_block, factors):
    left_side = left_block.astype(jnp.float32)
    right_side = right_block.astype(jnp.float32)
    real_part = jnp.einsum('fwi,fwj->fij', left_side[0], right_side[0]) + jnp.einsum('fwi,fwj->fij', left_side[1], right_side[1])
    imag_part = jnp.einsum('fwi,fwj->fij', left_side[1], right_side[0]) - jnp.einsum('fwi,fwj->fij', left_side[0], right_side[1])
    products = jnp.concatenate([real_part, imag_part], axis=0)
    flattened = products.reshape(products.shape[0], -1)
    return jnp.dot(factors, flattened, precision=lax.Precision.HIGHEST).reshape(LAGS, BLOCK, BLOCK)

def nothing(left_block, right_block, factors):
    return jnp.zeros((LAGS, BLOCK, BLOCK), jnp.float32)

def reference(spectra, valid_mask, pair_reach):
    values = spectra.astype(jnp.float32)
    energy = lax.optimization_barrier(jnp.sum(values[0] * values[0] + values[1] * values[1], axis=0)) / FREQS
    whitened = (values * (valid_mask.astype(jnp.float32) / jnp.sqrt(energy + 1e-06))).astype(jnp.bfloat16)
    factors = twiddles(jnp.arange(FREQS, dtype=jnp.float32), LAGS)
    block_count = NBLOCKS

    def one_block(block_index):
        start = (block_index * BLOCK).astype(jnp.int32)
        left_block = lax.dynamic_slice_in_dim(whitened, start, BLOCK, 3)
        results = []
        for offset in range(BAND + 1):
            other = jnp.minimum(block_index + offset, block_count - 1)
            right_block = lax.dynamic_slice_in_dim(whitened, (other * BLOCK).astype(jnp.int32), BLOCK, 3)
            usable = jnp.logical_and(offset <= pair_reach[block_index], block_index + offset < block_count)
            results.append(lax.cond(usable, correlate, nothing, left_block, right_block, factors))
        return jnp.stack(results)
    forward = lax.map(one_block, jnp.arange(block_count, dtype=jnp.int32))
    pieces = []
    for offset in range(BAND, 0, -1):
        moved = jnp.concatenate([jnp.zeros((offset,) + forward.shape[2:], jnp.float32), forward[:block_count - offset, offset]], axis=0)
        pieces.append(jnp.swapaxes(moved, -1, -2))
    for offset in range(BAND + 1):
        pieces.append(forward[:, offset])
    return jnp.stack(pieces, axis=1)
```

```python
import functools

import jax
import jax.numpy as jnp
import numpy as np
from jax import lax
from jax.experimental import pallas as pl
from jax.experimental.pallas import tpu as pltpu
from jax.sharding import PartitionSpec as P

FREQS = 512
BAND = 2
LAG_DEV = 1


first_bin = 64.0
lag_step = 24.0
transform_length = 2048.0


def shifted(block, axis, distance):
    devices = range(lax.axis_size(axis))
    route = [(i - distance, i) for i in devices if i - distance in devices]
    return lax.ppermute(block, axis, route)


def twiddles(bins, lag_count):
    lag_values = jnp.arange(lag_count, dtype=jnp.float32) * lag_step
    angle = 2.0 * jnp.pi / transform_length * lag_values[:, None] * (first_bin + bins)[None, :]
    paired = jnp.stack([jnp.cos(angle), -jnp.sin(angle)], axis=2)
    return paired.reshape(lag_count, 2 * bins.shape[0])


def left_form(block_data):
    upper_half = jnp.concatenate([block_data[0], block_data[1]], axis=1)
    lower_half = jnp.concatenate([block_data[1], -block_data[0]], axis=1)
    return jnp.stack([upper_half, lower_half], axis=1)


def right_form(block_data):
    return jnp.concatenate([block_data[0], block_data[1]], axis=1)


def correlate(left_side, right_side, factors):
    products = jnp.einsum(
        "fkwi,fwj->fkij", left_side, right_side, preferred_element_type=jnp.float32
    )
    flattened = products.reshape(2 * products.shape[0], -1)
    return jnp.dot(factors, flattened, precision=lax.Precision.HIGHEST)


def select_entry(table, position):
    positions = jnp.arange(table.shape[0], dtype=jnp.int32)
    return jnp.sum(jnp.where(positions == position, table, 0))


def spectra_from(block_data, offset):
    return shifted(block_data, "fiber", offset)


def result_from(lag_tile, offset):
    return shifted(lag_tile, "fiber", offset)


def spread(spectra, valid_mask, pair_reach):
    groups = lax.axis_size("freq")
    fibers = lax.axis_size("fiber")
    lag_count = LAG_DEV * groups
    masked = spectra * valid_mask.astype(jnp.bfloat16)
    raw_blocks = lax.all_to_all(masked, "fiber", split_axis=3, concat_axis=2, tiled=True)
    values = raw_blocks.astype(jnp.float32)
    energy = (
        lax.psum(jnp.sum(values[0] * values[0] + values[1] * values[1], axis=0), "freq") / FREQS
    )
    resident = (values / jnp.sqrt(energy + 1e-06)).astype(jnp.bfloat16)
    location = lax.axis_index("fiber")
    bin_count = resident.shape[1]
    bins = lax.axis_index("freq") * bin_count + jnp.arange(bin_count, dtype=jnp.int32)
    factors = twiddles(bins.astype(jnp.float32), lag_count)
    block = resident.shape[3]
    own_left = left_form(resident)

    def nothing(left_side, right_side, table_part):
        return jnp.zeros((lag_count, block * block), jnp.float32)

    partials = []
    for offset in range(BAND + 1):
        other = resident if offset == 0 else spectra_from(resident, -offset)
        usable = jnp.logical_and(
            offset <= select_entry(pair_reach, location), location + offset < fibers
        )
        partials.append(lax.cond(usable, correlate, nothing, own_left, right_form(other), factors))
    summed = lax.psum_scatter(jnp.stack(partials), "freq", scatter_dimension=1, tiled=True)
    forward = [summed[0]]
    backward = []
    for offset in range(1, BAND + 1):
        forward.append(summed[offset])
        backward.append(result_from(summed[offset], offset))
    tiles = []
    for lag_tile in backward[::-1]:
        shaped = lag_tile.reshape(lag_tile.shape[0], block, block)
        tiles.append(jnp.swapaxes(shaped, 1, 2))
    for lag_tile in forward:
        tiles.append(lag_tile.reshape(lag_tile.shape[0], block, block))
    return jnp.stack(tiles)[None]


CORE_BIT = 0
MESH = pl.DeviceIdType.MESH


def fused_kernel(dims, reach_ref, x_ref, mask_ref, wave_ref, out_ref, white, acc, core_in, tile_in,
                 energy_buf, edge_out, edge_in, core_send, core_recv, tile_send, tile_recv,
                 energy_send, energy_recv, edge_send, edge_recv):
    fibers, groups, block, bins, freqs = dims
    lag_count = groups * LAG_DEV
    fbits = fibers.bit_length() - 1
    gbits = groups.bit_length() - 1
    channels = fibers * block
    offsets = BAND + 1
    me = lax.axis_index("fiber")
    group = lax.axis_index("freq")

    def bit_of(value, k):
        return lax.rem(lax.div(value, 1 << k), 2)

    def partner(axis, k):
        place = me if axis == "fiber" else group
        return {axis: place + (1 - 2 * bit_of(place, k)) * (1 << k)}

    fiber_axes = [("fiber", k) for k in range(1, fbits)]
    freq_axes = [("freq", k) for k in range(gbits)]
    orders = [
        freq_axes + fiber_axes,
        fiber_axes[:1] + fiber_axes[1:] + freq_axes,
        fiber_axes[1:] + freq_axes + fiber_axes[:1],
    ]
    steps = len(freq_axes) + len(fiber_axes)

    def mine(axis):
        return bit_of(me if axis[0] == "fiber" else group, axis[1])

    def tile_place(relative):
        b = bit_of(me, CORE_BIT)
        lag = 0
        for axis, r in relative.items():
            own = mine(axis)
            value = r * own + (1 - r) * (1 - own)
            if axis[0] == "fiber":
                b = b + value * (1 << axis[1])
            else:
                lag = lag + value * (1 << axis[1])
        return b, lag

    def tile_copy(p, s, slot, b, lag):
        axis = orders[p][s]
        return pltpu.make_async_remote_copy(
            src_ref=acc.at[b, p, lag],
            dst_ref=tile_in.at[p, s, slot],
            send_sem=tile_send.at[p, s, slot],
            recv_sem=tile_recv.at[p, s, slot],
            device_id=partner(*axis),
            device_id_type=MESH,
        )

    def slot_of(p, s, relative):
        slot = 0
        for axis in orders[p][s + 1:]:
            slot = slot * 2 + relative[axis]
        return slot

    barrier = pltpu.get_barrier_semaphore()
    hyper = [("fiber", k) for k in range(fbits)] + freq_axes
    for axis in hyper:
        pl.semaphore_signal(barrier, inc=1, device_id=partner(*axis), device_id_type=MESH)
    near = [d for o in range(1, offsets) for d in (o, -o)]

    def inside(d):
        return jnp.logical_and(me + d >= 0, me + d < fibers)

    for d in near:
        @pl.when(inside(d))
        def _():
            pl.semaphore_signal(barrier, inc=1, device_id={"fiber": me + d}, device_id_type=MESH)

    rows = 64
    chunks = 2 * bins // rows

    def add_energy(i, total):
        part = x_ref[pl.ds(pl.multiple_of(i * rows, rows), rows), :].astype(jnp.float32)
        return total + jnp.sum(part * part, axis=0, keepdims=True)

    energy = lax.fori_loop(0, chunks, add_energy, jnp.zeros((1, channels), jnp.float32))
    peers = len(hyper)
    for d in near:
        peers = peers + jnp.where(inside(d), 1, 0)
    pl.semaphore_wait(barrier, peers)

    for k in range(gbits):
        energy_buf[2 * k] = energy
        copy = pltpu.make_async_remote_copy(
            src_ref=energy_buf.at[2 * k],
            dst_ref=energy_buf.at[2 * k + 1],
            send_sem=energy_send.at[k],
            recv_sem=energy_recv.at[k],
            device_id=partner("freq", k),
            device_id_type=MESH,
        )
        copy.start()
        copy.wait()
        energy = energy + energy_buf[2 * k + 1]
    scale = mask_ref[...].astype(jnp.float32) / jnp.sqrt(energy * (1.0 / freqs) + 1e-06)

    def whiten(i, carry):
        at = pl.ds(pl.multiple_of(i * rows, rows), rows)
        white[at, pl.ds(0, channels)] = (x_ref[at, :].astype(jnp.float32) * scale).astype(jnp.bfloat16)
        return carry

    lax.fori_loop(0, chunks, whiten, 0)
    white[:, pl.ds(channels, BAND * block)] = jnp.zeros((2 * bins, BAND * block), jnp.bfloat16)

    first = pl.multiple_of(group * bins, bins)

    def block_tiles(b):
        start = pl.multiple_of(b * block, block)
        turned = white[:, pl.ds(start, block)].astype(jnp.float32).T
        upper, lower = turned[:, :bins], turned[:, bins:]
        right = white[:, pl.ds(start, offsets * block)]
        for lag in range(lag_count):
            c = wave_ref[pl.ds(lag, 1), pl.ds(first, bins)]
            s = wave_ref[pl.ds(lag_count + lag, 1), pl.ds(first, bins)]
            rotated = jnp.concatenate([c * upper - s * lower, s * upper + c * lower], axis=1)
            high = rotated.astype(jnp.bfloat16)
            low = (rotated - high.astype(jnp.float32)).astype(jnp.bfloat16)
            both = jnp.dot(
                jnp.concatenate([high, low], axis=0), right, preferred_element_type=jnp.float32
            )
            both = both[:block] + both[block:]
            for d in range(offsets):
                acc[b, d, lag] = both[:, d * block:(d + 1) * block]

    halves = fibers // 2
    core = bit_of(me, CORE_BIT)
    order_bits = [axis for axis in fiber_axes[1:2] + fiber_axes[:1] + fiber_axes[2:]]

    def relatives(j):
        found = {}
        for i, axis in enumerate(order_bits):
            found[axis] = bit_of(j, len(order_bits) - 1 - i)
        return found

    def core_copy(j, b):
        return pltpu.make_async_remote_copy(
            src_ref=acc.at[b],
            dst_ref=core_in.at[j],
            send_sem=core_send.at[j],
            recv_sem=core_recv.at[j],
            device_id=partner("fiber", CORE_BIT),
            device_id_type=MESH,
        )

    def other_half(j, carry):
        b, _ = tile_place(relatives(j))
        b = b + 1 - 2 * core
        block_tiles(b)
        core_copy(j, b).start()
        return carry

    def own_half(j, carry):
        relative = relatives(j)
        b, _ = tile_place(relative)
        block_tiles(b)
        core_copy(j, b).wait_recv()
        acc[b] = acc[b] + core_in[j]
        for p in range(offsets):
            lead = orders[p][0]
            for choice in range(1 << gbits):
                full = dict(relative)
                for i, axis in enumerate(freq_axes):
                    full[axis] = (choice >> i) & 1
                if lead in freq_axes:
                    if full[lead] == 0:
                        tile_copy(p, 0, slot_of(p, 0, full), *tile_place(full)).start()
                else:
                    @pl.when(full[lead] == 0)
                    def _():
                        tile_copy(p, 0, slot_of(p, 0, full), *tile_place(full)).start()
        return carry

    lax.fori_loop(0, halves, other_half, 0)
    lax.fori_loop(0, halves, own_half, 0)

    for s in range(steps):
        for slot in range(1 << (steps - 1 - s)):
            for p in range(offsets):
                relative = {axis: 1 for axis in orders[p][: s + 1]}
                rest = orders[p][s + 1:]
                for i, axis in enumerate(rest):
                    relative[axis] = (slot >> (len(rest) - 1 - i)) & 1
                b, lag = tile_place(relative)
                tile_copy(p, s, slot, b, lag).wait_recv()
                acc[b, p, lag] = acc[b, p, lag] + tile_in[p, s, slot]
                if rest and relative[rest[0]] == 0:
                    tile_copy(p, s + 1, slot_of(p, s + 1, relative), b, lag).start()

    reach = reach_ref[me]

    def edge_copy(d):
        return pltpu.make_async_remote_copy(
            src_ref=edge_out.at[d - 1],
            dst_ref=edge_in.at[d - 1],
            send_sem=edge_send.at[d - 1],
            recv_sem=edge_recv.at[d - 1],
            device_id={"fiber": me + d},
            device_id_type=MESH,
        )

    for d in range(1, offsets):
        usable = jnp.where(jnp.logical_and(d <= reach, me + d < fibers), 1.0, 0.0)
        tile = acc[me, d, group] * usable
        out_ref[BAND + d] = tile
        edge_out[d - 1] = tile.T

        @pl.when(inside(d))
        def _():
            edge_copy(d).start()
    out_ref[BAND] = acc[me, 0, group]

    for d in range(1, offsets):
        out_ref[BAND - d] = jnp.zeros((block, block), jnp.float32)

        @pl.when(inside(-d))
        def _():
            edge_copy(d).wait_recv()
            out_ref[BAND - d] = edge_in[d - 1]

    for d in range(1, offsets):
        @pl.when(inside(d))
        def _():
            edge_copy(d).wait_send()

    def drain(j, carry):
        b, _ = tile_place(relatives(j))
        core_copy(j, b + 1 - 2 * core).wait_send()
        return carry

    lax.fori_loop(0, halves, drain, 0)
    for s in range(steps):
        for slot in range(1 << (steps - 1 - s)):
            for p in range(offsets):
                tile_copy(p, s, slot, me, 0).wait_send()


def fused(spectra, valid_mask, pair_reach):
    groups, fibers = lax.axis_size("freq"), lax.axis_size("fiber")
    bins, channels = spectra.shape[1], spectra.shape[3]
    block = channels // fibers
    freqs = bins * groups
    lag_count = groups * LAG_DEV
    offsets = BAND + 1
    angle = (
        2.0 * np.pi / transform_length * lag_step
        * np.arange(lag_count)[:, None] * (first_bin + np.arange(freqs))[None, :]
    )
    wave = jnp.asarray(np.concatenate([np.cos(angle), np.sin(angle)]).astype(np.float32))
    steps = (groups.bit_length() - 1) + (fibers.bit_length() - 2)
    slots = 1 << (steps - 1)
    tile = (block, block)
    vmem = pl.BlockSpec(memory_space=pltpu.VMEM)
    sem = pltpu.SemaphoreType.DMA
    result = pl.pallas_call(
        functools.partial(fused_kernel, (fibers, groups, block, bins, freqs)),
        out_shape=jax.ShapeDtypeStruct((2 * BAND + 1,) + tile, jnp.float32),
        in_specs=[pl.BlockSpec(memory_space=pltpu.SMEM), vmem, vmem, vmem],
        out_specs=vmem,
        scratch_shapes=[
            pltpu.VMEM((2 * bins, channels + BAND * block), jnp.bfloat16),
            pltpu.VMEM((fibers, offsets, lag_count) + tile, jnp.float32),
            pltpu.VMEM((fibers // 2, offsets, lag_count) + tile, jnp.float32),
            pltpu.VMEM((offsets, steps, slots) + tile, jnp.float32),
            pltpu.VMEM((2 * (groups.bit_length() - 1), 1, channels), jnp.float32),
            pltpu.VMEM((BAND,) + tile, jnp.float32),
            pltpu.VMEM((BAND,) + tile, jnp.float32),
            sem((fibers // 2,)), sem((fibers // 2,)),
            sem((offsets, steps, slots)), sem((offsets, steps, slots)),
            sem((groups.bit_length() - 1,)), sem((groups.bit_length() - 1,)),
            sem((BAND,)), sem((BAND,)),
        ],
        compiler_params=pltpu.CompilerParams(
            collective_id=0, has_side_effects=True, vmem_limit_bytes=48 * 1024 * 1024
        ),
    )(pair_reach, spectra.reshape(2 * bins, channels), valid_mask, wave)
    return result[None, :, None]


def power_of_two(n):
    return n & (n - 1) == 0


def fits_on_chip(fibers, groups, spectra):
    block = spectra.shape[3] // fibers
    partial_bytes = 4 * fibers * (BAND + 1) * groups * LAG_DEV * block * block
    return (
        power_of_two(fibers) and power_of_two(groups) and fibers >= 8 and groups >= 2
        and block % 128 == 0 and spectra.shape[1] % 128 == 0 and partial_bytes <= 1 << 23
    )


def shards(spectra, valid_mask, pair_reach):
    if fits_on_chip(lax.axis_size("fiber"), lax.axis_size("freq"), spectra):
        return fused(spectra, valid_mask, pair_reach)
    return spread(spectra, valid_mask, pair_reach)


def solution(mesh):
    return jax.shard_map(
        shards,
        mesh=mesh,
        in_specs=(P(None, "freq", "fiber", None), P("fiber", None), P()),
        out_specs=P("fiber", None, "freq", None, None),
        check_vma=False,
    )
```

```python
import functools

import jax
import jax.numpy as jnp
import numpy as np
from jax import lax
from jax.experimental import pallas as pl
from jax.experimental.pallas import tpu as pltpu
from jax.sharding import PartitionSpec as P

FREQS = 512
BAND = 2
LAG_DEV = 1


first_bin = 64.0
lag_step = 24.0
transform_length = 2048.0


def shifted(block, axis, distance):
    devices = range(lax.axis_size(axis))
    route = [(i - distance, i) for i in devices if i - distance in devices]
    return lax.ppermute(block, axis, route)


def twiddles(bins, lag_count):
    lag_values = jnp.arange(lag_count, dtype=jnp.float32) * lag_step
    angle = 2.0 * jnp.pi / transform_length * lag_values[:, None] * (first_bin + bins)[None, :]
    paired = jnp.stack([jnp.cos(angle), -jnp.sin(angle)], axis=2)
    return paired.reshape(lag_count, 2 * bins.shape[0])


def left_form(block_data):
    upper_half = jnp.concatenate([block_data[0], block_data[1]], axis=1)
    lower_half = jnp.concatenate([block_data[1], -block_data[0]], axis=1)
    return jnp.stack([upper_half, lower_half], axis=1)


def right_form(block_data):
    return jnp.concatenate([block_data[0], block_data[1]], axis=1)


def correlate(left_side, right_side, factors):
    products = jnp.einsum(
        "fkwi,fwj->fkij", left_side, right_side, preferred_element_type=jnp.float32
    )
    flattened = products.reshape(2 * products.shape[0], -1)
    return jnp.dot(factors, flattened, precision=lax.Precision.HIGHEST)


def select_entry(table, position):
    positions = jnp.arange(table.shape[0], dtype=jnp.int32)
    return jnp.sum(jnp.where(positions == position, table, 0))


def spectra_from(block_data, offset):
    return shifted(block_data, "fiber", offset)


def result_from(lag_tile, offset):
    return shifted(lag_tile, "fiber", offset)


def spread(spectra, valid_mask, pair_reach):
    groups = lax.axis_size("freq")
    fibers = lax.axis_size("fiber")
    lag_count = LAG_DEV * groups
    masked = spectra * valid_mask.astype(jnp.bfloat16)
    raw_blocks = lax.all_to_all(masked, "fiber", split_axis=3, concat_axis=2, tiled=True)
    values = raw_blocks.astype(jnp.float32)
    energy = (
        lax.psum(jnp.sum(values[0] * values[0] + values[1] * values[1], axis=0), "freq") / FREQS
    )
    resident = (values / jnp.sqrt(energy + 1e-06)).astype(jnp.bfloat16)
    location = lax.axis_index("fiber")
    bin_count = resident.shape[1]
    bins = lax.axis_index("freq") * bin_count + jnp.arange(bin_count, dtype=jnp.int32)
    factors = twiddles(bins.astype(jnp.float32), lag_count)
    block = resident.shape[3]
    own_left = left_form(resident)

    def nothing(left_side, right_side, table_part):
        return jnp.zeros((lag_count, block * block), jnp.float32)

    partials = []
    for offset in range(BAND + 1):
        other = resident if offset == 0 else spectra_from(resident, -offset)
        usable = jnp.logical_and(
            offset <= select_entry(pair_reach, location), location + offset < fibers
        )
        partials.append(lax.cond(usable, correlate, nothing, own_left, right_form(other), factors))
    summed = lax.psum_scatter(jnp.stack(partials), "freq", scatter_dimension=1, tiled=True)
    forward = [summed[0]]
    backward = []
    for offset in range(1, BAND + 1):
        forward.append(summed[offset])
        backward.append(result_from(summed[offset], offset))
    tiles = []
    for lag_tile in backward[::-1]:
        shaped = lag_tile.reshape(lag_tile.shape[0], block, block)
        tiles.append(jnp.swapaxes(shaped, 1, 2))
    for lag_tile in forward:
        tiles.append(lag_tile.reshape(lag_tile.shape[0], block, block))
    return jnp.stack(tiles)[None]


CORE_BIT = 0
MESH = pl.DeviceIdType.MESH


def fused_kernel(dims, reach_ref, x_ref, mask_ref, wave_ref, out_ref, white, acc, core_in, tile_in,
                 energy_buf, edge_out, edge_in, core_send, core_recv, tile_send, tile_recv,
                 energy_send, energy_recv, edge_send, edge_recv):
    fibers, groups, block, bins, freqs = dims
    lag_count = groups * LAG_DEV
    fbits = fibers.bit_length() - 1
    gbits = groups.bit_length() - 1
    channels = fibers * block
    offsets = BAND + 1
    me = lax.axis_index("fiber")
    group = lax.axis_index("freq")

    def bit_of(value, k):
        return lax.rem(lax.div(value, 1 << k), 2)

    def partner(axis, k):
        place = me if axis == "fiber" else group
        return {axis: place + (1 - 2 * bit_of(place, k)) * (1 << k)}

    fiber_axes = [("fiber", k) for k in range(1, fbits)]
    freq_axes = [("freq", k) for k in range(gbits)]
    near_axes, far_axes = fiber_axes[:1], fiber_axes[1:]
    orders = [
        freq_axes + near_axes + far_axes,
        near_axes + freq_axes + far_axes,
        freq_axes + far_axes + near_axes,
        near_axes + far_axes + freq_axes,
    ]
    orders = orders + orders[2:] * (offsets - 2)
    portions = list(range(2, 2 * offsets)) + [0, 1]
    half = block // 2
    steps = len(freq_axes) + len(fiber_axes)

    def mine(axis):
        return bit_of(me if axis[0] == "fiber" else group, axis[1])

    def tile_place(relative):
        b = bit_of(me, CORE_BIT)
        lag = 0
        for axis, r in relative.items():
            own = mine(axis)
            value = r * own + (1 - r) * (1 - own)
            if axis[0] == "fiber":
                b = b + value * (1 << axis[1])
            else:
                lag = lag + value * (1 << axis[1])
        return b, lag

    def half_of(p):
        return pl.ds((p % 2) * half, half)

    def place_in(s, slot):
        return (1 << steps) - (1 << (steps - s)) + slot

    def tile_copy(p, s, slot, b, lag):
        axis = orders[p][s]
        place = place_in(s, slot)
        return pltpu.make_async_remote_copy(
            src_ref=acc.at[b, p // 2, lag, half_of(p)],
            dst_ref=tile_in.at[p, place],
            send_sem=tile_send.at[p, place],
            recv_sem=tile_recv.at[p, place],
            device_id=partner(*axis),
            device_id_type=MESH,
        )

    def slot_of(p, s, relative):
        slot = 0
        for axis in orders[p][s + 1:]:
            slot = slot * 2 + relative[axis]
        return slot

    barrier = pltpu.get_barrier_semaphore()
    hyper = [("fiber", k) for k in range(fbits)] + freq_axes
    for axis in hyper:
        pl.semaphore_signal(barrier, inc=1, device_id=partner(*axis), device_id_type=MESH)
    near = [d for o in range(1, offsets) for d in (o, -o)]

    def inside(d):
        return jnp.logical_and(me + d >= 0, me + d < fibers)

    for d in near:
        @pl.when(inside(d))
        def _():
            pl.semaphore_signal(barrier, inc=1, device_id={"fiber": me + d}, device_id_type=MESH)

    rows = 64
    chunks = 2 * bins // rows

    def add_energy(i, total):
        part = x_ref[pl.ds(pl.multiple_of(i * rows, rows), rows), :].astype(jnp.float32)
        return total + jnp.sum(part * part, axis=0, keepdims=True)

    energy = lax.fori_loop(0, chunks, add_energy, jnp.zeros((1, channels), jnp.float32))
    peers = len(hyper)
    for d in near:
        peers = peers + jnp.where(inside(d), 1, 0)
    pl.semaphore_wait(barrier, peers)

    for k in range(gbits):
        energy_buf[2 * k] = energy
        copy = pltpu.make_async_remote_copy(
            src_ref=energy_buf.at[2 * k],
            dst_ref=energy_buf.at[2 * k + 1],
            send_sem=energy_send.at[k],
            recv_sem=energy_recv.at[k],
            device_id=partner("freq", k),
            device_id_type=MESH,
        )
        copy.start()
        copy.wait()
        energy = energy + energy_buf[2 * k + 1]
    scale = mask_ref[...].astype(jnp.float32) / jnp.sqrt(energy * (1.0 / freqs) + 1e-06)

    def whiten(i, carry):
        at = pl.ds(pl.multiple_of(i * rows, rows), rows)
        white[at, pl.ds(0, channels)] = (x_ref[at, :].astype(jnp.float32) * scale).astype(jnp.bfloat16)
        return carry

    lax.fori_loop(0, chunks, whiten, 0)
    white[:, pl.ds(channels, BAND * block)] = jnp.zeros((2 * bins, BAND * block), jnp.bfloat16)

    first = pl.multiple_of(group * bins, bins)

    def block_tiles(b):
        start = pl.multiple_of(b * block, block)
        turned = white[:, pl.ds(start, block)].astype(jnp.float32).T
        upper, lower = turned[:, :bins], turned[:, bins:]
        right = white[:, pl.ds(start, offsets * block)]
        for lag in range(lag_count):
            c = wave_ref[pl.ds(lag, 1), pl.ds(first, bins)]
            s = wave_ref[pl.ds(lag_count + lag, 1), pl.ds(first, bins)]
            rotated = jnp.concatenate([c * upper - s * lower, s * upper + c * lower], axis=1)
            high = rotated.astype(jnp.bfloat16)
            low = (rotated - high.astype(jnp.float32)).astype(jnp.bfloat16)
            both = jnp.dot(
                jnp.concatenate([high, low], axis=0), right, preferred_element_type=jnp.float32
            )
            both = both[:block] + both[block:]
            for d in range(offsets):
                acc[b, d, lag] = both[:, d * block:(d + 1) * block]

    halves = fibers // 2
    core = bit_of(me, CORE_BIT)
    order_bits = near_axes + far_axes

    def relatives(j):
        found = {}
        for i, axis in enumerate(order_bits):
            found[axis] = bit_of(j, len(order_bits) - 1 - i)
        return found

    def core_copy(j, b):
        return pltpu.make_async_remote_copy(
            src_ref=acc.at[b],
            dst_ref=core_in.at[j],
            send_sem=core_send.at[j],
            recv_sem=core_recv.at[j],
            device_id=partner("fiber", CORE_BIT),
            device_id_type=MESH,
        )

    def finish(j):
        relative = relatives(j)
        b, _ = tile_place(relative)
        core_copy(j, b).wait_recv()
        acc[b] = acc[b] + core_in[j]
        for p in portions:
            lead = orders[p][0]
            for choice in range(1 << gbits):
                full = dict(relative)
                for i, axis in enumerate(freq_axes):
                    full[axis] = (choice >> i) & 1
                if lead in freq_axes:
                    if full[lead] == 0:
                        tile_copy(p, 0, slot_of(p, 0, full), *tile_place(full)).start()
                else:
                    @pl.when(full[lead] == 0)
                    def _():
                        tile_copy(p, 0, slot_of(p, 0, full), *tile_place(full)).start()

    def two_blocks(j, carry):
        b, _ = tile_place(relatives(j))
        other = b + 1 - 2 * core
        block_tiles(other)
        core_copy(j, other).start()

        @pl.when(j > 0)
        def _():
            finish(j - 1)

        block_tiles(b)
        return carry

    lax.fori_loop(0, halves, two_blocks, 0)
    finish(halves - 1)

    for s in range(steps):
        for slot in range(1 << (steps - 1 - s)):
            for p in portions:
                relative = {axis: 1 for axis in orders[p][: s + 1]}
                rest = orders[p][s + 1:]
                for i, axis in enumerate(rest):
                    relative[axis] = (slot >> (len(rest) - 1 - i)) & 1
                b, lag = tile_place(relative)
                tile_copy(p, s, slot, b, lag).wait_recv()
                part = acc[b, p // 2, lag, half_of(p)]
                acc[b, p // 2, lag, half_of(p)] = part + tile_in[p, place_in(s, slot)]
                if rest and relative[rest[0]] == 0:
                    tile_copy(p, s + 1, slot_of(p, s + 1, relative), b, lag).start()

    reach = reach_ref[me]

    def edge_copy(d):
        return pltpu.make_async_remote_copy(
            src_ref=edge_out.at[d - 1],
            dst_ref=edge_in.at[d - 1],
            send_sem=edge_send.at[d - 1],
            recv_sem=edge_recv.at[d - 1],
            device_id={"fiber": me + d},
            device_id_type=MESH,
        )

    for d in range(1, offsets):
        usable = jnp.where(jnp.logical_and(d <= reach, me + d < fibers), 1.0, 0.0)
        tile = acc[me, d, group] * usable
        out_ref[BAND + d] = tile
        edge_out[d - 1] = tile.T

        @pl.when(inside(d))
        def _():
            edge_copy(d).start()
    out_ref[BAND] = acc[me, 0, group]

    for d in range(1, offsets):
        out_ref[BAND - d] = jnp.zeros((block, block), jnp.float32)

        @pl.when(inside(-d))
        def _():
            edge_copy(d).wait_recv()
            out_ref[BAND - d] = edge_in[d - 1]

    for d in range(1, offsets):
        @pl.when(inside(d))
        def _():
            edge_copy(d).wait_send()

    def drain(j, carry):
        b, _ = tile_place(relatives(j))
        core_copy(j, b + 1 - 2 * core).wait_send()
        return carry

    lax.fori_loop(0, halves, drain, 0)
    for s in range(steps):
        for slot in range(1 << (steps - 1 - s)):
            for p in portions:
                tile_copy(p, s, slot, me, 0).wait_send()


def fused(spectra, valid_mask, pair_reach):
    groups, fibers = lax.axis_size("freq"), lax.axis_size("fiber")
    bins, channels = spectra.shape[1], spectra.shape[3]
    block = channels // fibers
    freqs = bins * groups
    lag_count = groups * LAG_DEV
    offsets = BAND + 1
    angle = (
        2.0 * np.pi / transform_length * lag_step
        * np.arange(lag_count)[:, None] * (first_bin + np.arange(freqs))[None, :]
    )
    wave = jnp.asarray(np.concatenate([np.cos(angle), np.sin(angle)]).astype(np.float32))
    steps = (groups.bit_length() - 1) + (fibers.bit_length() - 2)
    slots = (1 << steps) - 1
    tile = (block, block)
    vmem = pl.BlockSpec(memory_space=pltpu.VMEM)
    sem = pltpu.SemaphoreType.DMA
    result = pl.pallas_call(
        functools.partial(fused_kernel, (fibers, groups, block, bins, freqs)),
        out_shape=jax.ShapeDtypeStruct((2 * BAND + 1,) + tile, jnp.float32),
        in_specs=[pl.BlockSpec(memory_space=pltpu.SMEM), vmem, vmem, vmem],
        out_specs=vmem,
        scratch_shapes=[
            pltpu.VMEM((2 * bins, channels + BAND * block), jnp.bfloat16),
            pltpu.VMEM((fibers, offsets, lag_count) + tile, jnp.float32),
            pltpu.VMEM((fibers // 2, offsets, lag_count) + tile, jnp.float32),
            pltpu.VMEM((2 * offsets, slots, block // 2, block), jnp.float32),
            pltpu.VMEM((2 * (groups.bit_length() - 1), 1, channels), jnp.float32),
            pltpu.VMEM((BAND,) + tile, jnp.float32),
            pltpu.VMEM((BAND,) + tile, jnp.float32),
            sem((fibers // 2,)), sem((fibers // 2,)),
            sem((2 * offsets, slots)), sem((2 * offsets, slots)),
            sem((groups.bit_length() - 1,)), sem((groups.bit_length() - 1,)),
            sem((BAND,)), sem((BAND,)),
        ],
        compiler_params=pltpu.CompilerParams(
            collective_id=0, has_side_effects=True, vmem_limit_bytes=48 * 1024 * 1024
        ),
    )(pair_reach, spectra.reshape(2 * bins, channels), valid_mask, wave)
    return result[None, :, None]


def power_of_two(n):
    return n & (n - 1) == 0


def fits_on_chip(fibers, groups, spectra):
    block = spectra.shape[3] // fibers
    partial_bytes = 4 * fibers * (BAND + 1) * groups * LAG_DEV * block * block
    return (
        power_of_two(fibers) and power_of_two(groups) and fibers >= 8 and groups >= 2
        and block % 128 == 0 and spectra.shape[1] % 128 == 0 and partial_bytes <= 1 << 23
    )


def shards(spectra, valid_mask, pair_reach):
    if fits_on_chip(lax.axis_size("fiber"), lax.axis_size("freq"), spectra):
        return fused(spectra, valid_mask, pair_reach)
    return spread(spectra, valid_mask, pair_reach)


def solution(mesh):
    return jax.shard_map(
        shards,
        mesh=mesh,
        in_specs=(P(None, "freq", "fiber", None), P("fiber", None), P()),
        out_specs=P("fiber", None, "freq", None, None),
        check_vma=False,
    )
```

```python
import functools

import jax
import jax.numpy as jnp
import numpy as np
from jax import lax
from jax.experimental import pallas as pl
from jax.experimental.pallas import tpu as pltpu
from jax.sharding import PartitionSpec as P

FREQS = 512
BAND = 2
LAG_DEV = 1


first_bin = 64.0
lag_step = 24.0
transform_length = 2048.0


def shifted(block, axis, distance):
    devices = range(lax.axis_size(axis))
    route = [(i - distance, i) for i in devices if i - distance in devices]
    return lax.ppermute(block, axis, route)


def twiddles(bins, lag_count):
    lag_values = jnp.arange(lag_count, dtype=jnp.float32) * lag_step
    angle = 2.0 * jnp.pi / transform_length * lag_values[:, None] * (first_bin + bins)[None, :]
    paired = jnp.stack([jnp.cos(angle), -jnp.sin(angle)], axis=2)
    return paired.reshape(lag_count, 2 * bins.shape[0])


def left_form(block_data):
    upper_half = jnp.concatenate([block_data[0], block_data[1]], axis=1)
    lower_half = jnp.concatenate([block_data[1], -block_data[0]], axis=1)
    return jnp.stack([upper_half, lower_half], axis=1)


def right_form(block_data):
    return jnp.concatenate([block_data[0], block_data[1]], axis=1)


def correlate(left_side, right_side, factors):
    products = jnp.einsum(
        "fkwi,fwj->fkij", left_side, right_side, preferred_element_type=jnp.float32
    )
    flattened = products.reshape(2 * products.shape[0], -1)
    return jnp.dot(factors, flattened, precision=lax.Precision.HIGHEST)


def select_entry(table, position):
    positions = jnp.arange(table.shape[0], dtype=jnp.int32)
    return jnp.sum(jnp.where(positions == position, table, 0))


def spectra_from(block_data, offset):
    return shifted(block_data, "fiber", offset)


def result_from(lag_tile, offset):
    return shifted(lag_tile, "fiber", offset)


def spread(spectra, valid_mask, pair_reach):
    groups = lax.axis_size("freq")
    fibers = lax.axis_size("fiber")
    lag_count = LAG_DEV * groups
    masked = spectra * valid_mask.astype(jnp.bfloat16)
    raw_blocks = lax.all_to_all(masked, "fiber", split_axis=3, concat_axis=2, tiled=True)
    values = raw_blocks.astype(jnp.float32)
    energy = (
        lax.psum(jnp.sum(values[0] * values[0] + values[1] * values[1], axis=0), "freq") / FREQS
    )
    resident = (values / jnp.sqrt(energy + 1e-06)).astype(jnp.bfloat16)
    location = lax.axis_index("fiber")
    bin_count = resident.shape[1]
    bins = lax.axis_index("freq") * bin_count + jnp.arange(bin_count, dtype=jnp.int32)
    factors = twiddles(bins.astype(jnp.float32), lag_count)
    block = resident.shape[3]
    own_left = left_form(resident)

    def nothing(left_side, right_side, table_part):
        return jnp.zeros((lag_count, block * block), jnp.float32)

    partials = []
    for offset in range(BAND + 1):
        other = resident if offset == 0 else spectra_from(resident, -offset)
        usable = jnp.logical_and(
            offset <= select_entry(pair_reach, location), location + offset < fibers
        )
        partials.append(lax.cond(usable, correlate, nothing, own_left, right_form(other), factors))
    summed = lax.psum_scatter(jnp.stack(partials), "freq", scatter_dimension=1, tiled=True)
    forward = [summed[0]]
    backward = []
    for offset in range(1, BAND + 1):
        forward.append(summed[offset])
        backward.append(result_from(summed[offset], offset))
    tiles = []
    for lag_tile in backward[::-1]:
        shaped = lag_tile.reshape(lag_tile.shape[0], block, block)
        tiles.append(jnp.swapaxes(shaped, 1, 2))
    for lag_tile in forward:
        tiles.append(lag_tile.reshape(lag_tile.shape[0], block, block))
    return jnp.stack(tiles)[None]


CORE_BIT = 0
TURN, HOP = 2, 3
LOAD_ROWS = 64
PORTIONS = ("zxy", "zyx", "xyz", "yxz", "xyz", "yxz")
MESH = pl.DeviceIdType.MESH


def fused_kernel(dims, reach_hbm, x_hbm, mask_hbm, wave_hbm, out_ref, reach_ref, x_ref, mask_ref, wave_ref,
                 load_sem, small_sem, white, acc, core_in, tile_in,
                 energy_buf, edge_out, edge_in, core_send, core_recv, tile_send, tile_recv,
                 energy_send, energy_recv, edge_send, edge_recv):
    fibers, groups, block, bins, freqs = dims
    lag_count = groups * LAG_DEV
    fbits = fibers.bit_length() - 1
    gbits = groups.bit_length() - 1
    channels = fibers * block
    offsets = BAND + 1
    me = lax.axis_index("fiber")
    group = lax.axis_index("freq")

    def bit_of(value, k):
        return lax.rem(lax.div(value, 1 << k), 2)

    def partner(axis, k):
        place = me if axis == "fiber" else group
        return {axis: place + (1 - 2 * bit_of(place, k)) * (1 << k)}

    fiber_axes = [("fiber", k) for k in range(1, fbits)]
    freq_axes = [("freq", k) for k in range(gbits)]
    near_axes, far_axes = fiber_axes[:1], fiber_axes[1:]
    named = {"x": freq_axes, "y": near_axes, "z": far_axes}
    orders = [sum((named[n] for n in names), []) for names in PORTIONS]
    portions = list(range(2 * offsets))
    half = block // 2
    steps = len(freq_axes) + len(fiber_axes)

    def mine(axis):
        return bit_of(me if axis[0] == "fiber" else group, axis[1])

    def tile_place(relative):
        b = bit_of(me, CORE_BIT)
        lag = 0
        for axis, r in relative.items():
            own = mine(axis)
            value = r * own + (1 - r) * (1 - own)
            if axis[0] == "fiber":
                b = b + value * (1 << axis[1])
            else:
                lag = lag + value * (1 << axis[1])
        return b, lag

    def half_of(p):
        return pl.ds((p % 2) * half, half)

    def place_in(s, slot):
        return (1 << steps) - (1 << (steps - s)) + slot

    def tile_copy(p, s, slot, b, lag):
        axis = orders[p][s]
        place = place_in(s, slot)
        return pltpu.make_async_remote_copy(
            src_ref=acc.at[b, p // 2, lag, half_of(p)],
            dst_ref=tile_in.at[p, place],
            send_sem=tile_send.at[p, place],
            recv_sem=tile_recv.at[p, place],
            device_id=partner(*axis),
            device_id_type=MESH,
        )

    def slot_of(p, s, relative):
        slot = 0
        for axis in orders[p][s + 1:]:
            slot = slot * 2 + relative[axis]
        return slot

    rows = LOAD_ROWS
    chunks = 2 * bins // rows

    def load(i):
        at = pl.ds(pl.multiple_of(i * rows, rows), rows)
        return pltpu.make_async_copy(x_hbm.at[at], x_ref.at[at], load_sem.at[i])

    small = [
        pltpu.make_async_copy(source, target, small_sem.at[i])
        for i, (source, target) in enumerate(
            [(mask_hbm, mask_ref), (wave_hbm, wave_ref), (reach_hbm, reach_ref)]
        )
    ]
    for i in range(chunks):
        load(i).start()
    for copy in small:
        copy.start()

    barrier = pltpu.get_barrier_semaphore()
    hyper = [("fiber", k) for k in range(fbits)] + freq_axes
    for axis in hyper:
        pl.semaphore_signal(barrier, inc=1, device_id=partner(*axis), device_id_type=MESH)
    near = [d for o in range(1, offsets) for d in (o, -o)]

    def inside(d):
        return jnp.logical_and(me + d >= 0, me + d < fibers)

    for d in near:
        @pl.when(inside(d))
        def _():
            pl.semaphore_signal(barrier, inc=1, device_id={"fiber": me + d}, device_id_type=MESH)

    white[:, pl.ds(channels, BAND * block)] = jnp.zeros((2 * bins, BAND * block), jnp.bfloat16)

    def add_energy(i, total):
        load(i).wait()
        part = x_ref[pl.ds(pl.multiple_of(i * rows, rows), rows), :].astype(jnp.float32)
        return total + jnp.sum(part * part, axis=0, keepdims=True)

    energy = lax.fori_loop(0, chunks, add_energy, jnp.zeros((1, channels), jnp.float32))
    peers = len(hyper)
    for d in near:
        peers = peers + jnp.where(inside(d), 1, 0)
    pl.semaphore_wait(barrier, peers)

    for copy in small:
        copy.wait()
    for k in range(gbits):
        energy_buf[2 * k] = energy
        copy = pltpu.make_async_remote_copy(
            src_ref=energy_buf.at[2 * k],
            dst_ref=energy_buf.at[2 * k + 1],
            send_sem=energy_send.at[k],
            recv_sem=energy_recv.at[k],
            device_id=partner("freq", k),
            device_id_type=MESH,
        )
        copy.start()
        copy.wait()
        energy = energy + energy_buf[2 * k + 1]
    scale = mask_ref[...].astype(jnp.float32) / jnp.sqrt(energy * (1.0 / freqs) + 1e-06)

    def whiten(i, carry):
        at = pl.ds(pl.multiple_of(i * rows, rows), rows)
        white[at, pl.ds(0, channels)] = (x_ref[at, :].astype(jnp.float32) * scale).astype(jnp.bfloat16)
        return carry

    lax.fori_loop(0, chunks, whiten, 0)

    first = pl.multiple_of(group * bins, bins)

    def block_tiles(b):
        start = pl.multiple_of(b * block, block)
        turned = white[:, pl.ds(start, block)].astype(jnp.float32).T
        upper, lower = turned[:, :bins], turned[:, bins:]
        right = white[:, pl.ds(start, offsets * block)]
        for lag in range(lag_count):
            c = wave_ref[pl.ds(lag, 1), pl.ds(first, bins)]
            s = wave_ref[pl.ds(lag_count + lag, 1), pl.ds(first, bins)]
            rotated = jnp.concatenate([c * upper - s * lower, s * upper + c * lower], axis=1)
            high = rotated.astype(jnp.bfloat16)
            low = (rotated - high.astype(jnp.float32)).astype(jnp.bfloat16)
            both = jnp.dot(
                jnp.concatenate([high, low], axis=0), right, preferred_element_type=jnp.float32
            )
            both = both[:block] + both[block:]
            for d in range(offsets):
                acc[b, d, lag] = both[:, d * block:(d + 1) * block]

    halves = fibers // 2
    core = bit_of(me, CORE_BIT)
    order_bits = near_axes + far_axes

    def relatives(j):
        found = {}
        for i, axis in enumerate(order_bits):
            found[axis] = bit_of(j, len(order_bits) - 1 - i)
        return found

    def core_copy(j, b):
        return pltpu.make_async_remote_copy(
            src_ref=acc.at[b],
            dst_ref=core_in.at[j],
            send_sem=core_send.at[j],
            recv_sem=core_recv.at[j],
            device_id=partner("fiber", CORE_BIT),
            device_id_type=MESH,
        )

    def finish(j):
        relative = relatives(j)
        b, _ = tile_place(relative)
        core_copy(j, b).wait_recv()
        acc[b] = acc[b] + core_in[j]
        for p in portions:
            lead = orders[p][0]
            for choice in range(1 << gbits):
                full = dict(relative)
                for i, axis in enumerate(freq_axes):
                    full[axis] = (choice >> i) & 1
                if lead in freq_axes:
                    if full[lead] == 0:
                        tile_copy(p, 0, slot_of(p, 0, full), *tile_place(full)).start()
                else:
                    @pl.when(full[lead] == 0)
                    def _():
                        tile_copy(p, 0, slot_of(p, 0, full), *tile_place(full)).start()

    def two_blocks(j, carry):
        b, _ = tile_place(relatives(j))
        other = b + 1 - 2 * core
        block_tiles(other)
        core_copy(j, other).start()

        @pl.when(j > 0)
        def _():
            finish(j - 1)

        block_tiles(b)
        return carry

    lax.fori_loop(0, halves, two_blocks, 0)
    finish(halves - 1)

    def ready(p, s, relative):
        if s < 0:
            turn = 0
            for axis in order_bits:
                turn = 2 * turn + relative[axis]
            return turn * TURN
        axis = orders[p][s]
        sent = ready(p, s - 1, {**relative, axis: 0}) + HOP
        return max(sent, ready(p, s - 1, {**relative, axis: 1}))

    events = []
    for s in range(steps):
        for slot in range(1 << (steps - 1 - s)):
            for p in portions:
                rest = orders[p][s + 1:]
                relative = {axis: 1 for axis in orders[p][: s + 1]}
                for i, axis in enumerate(rest):
                    relative[axis] = (slot >> (len(rest) - 1 - i)) & 1
                events.append((ready(p, s, relative), s, len(events), p, slot, relative))
    for _, s, _, p, slot, relative in sorted(events, key=lambda event: event[:3]):
        rest = orders[p][s + 1:]
        b, lag = tile_place(relative)
        tile_copy(p, s, slot, b, lag).wait_recv()
        part = acc[b, p // 2, lag, half_of(p)]
        acc[b, p // 2, lag, half_of(p)] = part + tile_in[p, place_in(s, slot)]
        if rest and relative[rest[0]] == 0:
            tile_copy(p, s + 1, slot_of(p, s + 1, relative), b, lag).start()

    reach = reach_ref[me]

    def edge_copy(d):
        return pltpu.make_async_remote_copy(
            src_ref=edge_out.at[d - 1],
            dst_ref=edge_in.at[d - 1],
            send_sem=edge_send.at[d - 1],
            recv_sem=edge_recv.at[d - 1],
            device_id={"fiber": me + d},
            device_id_type=MESH,
        )

    for d in range(1, offsets):
        usable = jnp.where(jnp.logical_and(d <= reach, me + d < fibers), 1.0, 0.0)
        tile = acc[me, d, group] * usable
        out_ref[BAND + d] = tile
        edge_out[d - 1] = tile.T

        @pl.when(inside(d))
        def _():
            edge_copy(d).start()
    out_ref[BAND] = acc[me, 0, group]

    for d in range(1, offsets):
        out_ref[BAND - d] = jnp.zeros((block, block), jnp.float32)

        @pl.when(inside(-d))
        def _():
            edge_copy(d).wait_recv()
            out_ref[BAND - d] = edge_in[d - 1]

    for d in range(1, offsets):
        @pl.when(inside(d))
        def _():
            edge_copy(d).wait_send()

    def drain(j, carry):
        b, _ = tile_place(relatives(j))
        core_copy(j, b + 1 - 2 * core).wait_send()
        return carry

    lax.fori_loop(0, halves, drain, 0)
    for s in range(steps):
        for slot in range(1 << (steps - 1 - s)):
            for p in portions:
                tile_copy(p, s, slot, me, 0).wait_send()


def fused(spectra, valid_mask, pair_reach):
    groups, fibers = lax.axis_size("freq"), lax.axis_size("fiber")
    bins, channels = spectra.shape[1], spectra.shape[3]
    block = channels // fibers
    freqs = bins * groups
    lag_count = groups * LAG_DEV
    offsets = BAND + 1
    angle = (
        2.0 * np.pi / transform_length * lag_step
        * np.arange(lag_count)[:, None] * (first_bin + np.arange(freqs))[None, :]
    )
    wave = jnp.asarray(np.concatenate([np.cos(angle), np.sin(angle)]).astype(np.float32))
    steps = (groups.bit_length() - 1) + (fibers.bit_length() - 2)
    slots = (1 << steps) - 1
    tile = (block, block)
    vmem = pl.BlockSpec(memory_space=pltpu.VMEM)
    sem = pltpu.SemaphoreType.DMA
    result = pl.pallas_call(
        functools.partial(fused_kernel, (fibers, groups, block, bins, freqs)),
        out_shape=jax.ShapeDtypeStruct((2 * BAND + 1,) + tile, jnp.float32),
        in_specs=[pl.BlockSpec(memory_space=pl.ANY)] * 4,
        out_specs=vmem,
        scratch_shapes=[
            pltpu.SMEM(pair_reach.shape, jnp.int32),
            pltpu.VMEM((2 * bins, channels), jnp.bfloat16),
            pltpu.VMEM(valid_mask.shape, jnp.int32),
            pltpu.VMEM(wave.shape, jnp.float32),
            sem((2 * bins // LOAD_ROWS,)), sem((3,)),
            pltpu.VMEM((2 * bins, channels + BAND * block), jnp.bfloat16),
            pltpu.VMEM((fibers, offsets, lag_count) + tile, jnp.float32),
            pltpu.VMEM((fibers // 2, offsets, lag_count) + tile, jnp.float32),
            pltpu.VMEM((2 * offsets, slots, block // 2, block), jnp.float32),
            pltpu.VMEM((2 * (groups.bit_length() - 1), 1, channels), jnp.float32),
            pltpu.VMEM((BAND,) + tile, jnp.float32),
            pltpu.VMEM((BAND,) + tile, jnp.float32),
            sem((fibers // 2,)), sem((fibers // 2,)),
            sem((2 * offsets, slots)), sem((2 * offsets, slots)),
            sem((groups.bit_length() - 1,)), sem((groups.bit_length() - 1,)),
            sem((BAND,)), sem((BAND,)),
        ],
        compiler_params=pltpu.CompilerParams(
            collective_id=0, has_side_effects=True, vmem_limit_bytes=60 * 1024 * 1024
        ),
    )(pair_reach, spectra.reshape(2 * bins, channels), valid_mask, wave)
    return result[None, :, None]


def power_of_two(n):
    return n & (n - 1) == 0


def fits_on_chip(fibers, groups, spectra):
    block = spectra.shape[3] // fibers
    partial_bytes = 4 * fibers * (BAND + 1) * groups * LAG_DEV * block * block
    return (
        power_of_two(fibers) and power_of_two(groups) and fibers >= 8 and groups >= 2
        and block % 128 == 0 and spectra.shape[1] % 128 == 0 and partial_bytes <= 1 << 23
    )


def shards(spectra, valid_mask, pair_reach):
    if fits_on_chip(lax.axis_size("fiber"), lax.axis_size("freq"), spectra):
        return fused(spectra, valid_mask, pair_reach)
    return spread(spectra, valid_mask, pair_reach)


def solution(mesh):
    return jax.shard_map(
        shards,
        mesh=mesh,
        in_specs=(P(None, "freq", "fiber", None), P("fiber", None), P()),
        out_specs=P("fiber", None, "freq", None, None),
        check_vma=False,
    )
```

```python
import functools

import jax
import jax.numpy as jnp
import numpy as np
from jax import lax
from jax.experimental import pallas as pl
from jax.experimental.pallas import tpu as pltpu
from jax.sharding import PartitionSpec as P

FREQS = 512
BAND = 2
LAG_DEV = 1


first_bin = 64.0
lag_step = 24.0
transform_length = 2048.0


def shifted(block, axis, distance):
    devices = range(lax.axis_size(axis))
    route = [(i - distance, i) for i in devices if i - distance in devices]
    return lax.ppermute(block, axis, route)


def twiddles(bins, lag_count):
    lag_values = jnp.arange(lag_count, dtype=jnp.float32) * lag_step
    angle = 2.0 * jnp.pi / transform_length * lag_values[:, None] * (first_bin + bins)[None, :]
    paired = jnp.stack([jnp.cos(angle), -jnp.sin(angle)], axis=2)
    return paired.reshape(lag_count, 2 * bins.shape[0])


def left_form(block_data):
    upper_half = jnp.concatenate([block_data[0], block_data[1]], axis=1)
    lower_half = jnp.concatenate([block_data[1], -block_data[0]], axis=1)
    return jnp.stack([upper_half, lower_half], axis=1)


def right_form(block_data):
    return jnp.concatenate([block_data[0], block_data[1]], axis=1)


def correlate(left_side, right_side, factors):
    products = jnp.einsum(
        "fkwi,fwj->fkij", left_side, right_side, preferred_element_type=jnp.float32
    )
    flattened = products.reshape(2 * products.shape[0], -1)
    return jnp.dot(factors, flattened, precision=lax.Precision.HIGHEST)


def select_entry(table, position):
    positions = jnp.arange(table.shape[0], dtype=jnp.int32)
    return jnp.sum(jnp.where(positions == position, table, 0))


def spectra_from(block_data, offset):
    return shifted(block_data, "fiber", offset)


def result_from(lag_tile, offset):
    return shifted(lag_tile, "fiber", offset)


def spread(spectra, valid_mask, pair_reach):
    groups = lax.axis_size("freq")
    fibers = lax.axis_size("fiber")
    lag_count = LAG_DEV * groups
    masked = spectra * valid_mask.astype(jnp.bfloat16)
    raw_blocks = lax.all_to_all(masked, "fiber", split_axis=3, concat_axis=2, tiled=True)
    values = raw_blocks.astype(jnp.float32)
    energy = (
        lax.psum(jnp.sum(values[0] * values[0] + values[1] * values[1], axis=0), "freq") / FREQS
    )
    resident = (values / jnp.sqrt(energy + 1e-06)).astype(jnp.bfloat16)
    location = lax.axis_index("fiber")
    bin_count = resident.shape[1]
    bins = lax.axis_index("freq") * bin_count + jnp.arange(bin_count, dtype=jnp.int32)
    factors = twiddles(bins.astype(jnp.float32), lag_count)
    block = resident.shape[3]
    own_left = left_form(resident)

    def nothing(left_side, right_side, table_part):
        return jnp.zeros((lag_count, block * block), jnp.float32)

    partials = []
    for offset in range(BAND + 1):
        other = resident if offset == 0 else spectra_from(resident, -offset)
        usable = jnp.logical_and(
            offset <= select_entry(pair_reach, location), location + offset < fibers
        )
        partials.append(lax.cond(usable, correlate, nothing, own_left, right_form(other), factors))
    summed = lax.psum_scatter(jnp.stack(partials), "freq", scatter_dimension=1, tiled=True)
    forward = [summed[0]]
    backward = []
    for offset in range(1, BAND + 1):
        forward.append(summed[offset])
        backward.append(result_from(summed[offset], offset))
    tiles = []
    for lag_tile in backward[::-1]:
        shaped = lag_tile.reshape(lag_tile.shape[0], block, block)
        tiles.append(jnp.swapaxes(shaped, 1, 2))
    for lag_tile in forward:
        tiles.append(lag_tile.reshape(lag_tile.shape[0], block, block))
    return jnp.stack(tiles)[None]


CORE_BIT = 0
TURN, HOP = 2, 6
LOAD_ROWS = 64
PORTIONS = ("zxy", "zyx", "xyz", "yxz", "xyz", "yxz")
MESH = pl.DeviceIdType.MESH


def fused_kernel(dims, reach_hbm, x_hbm, mask_hbm, wave_hbm, out_ref, reach_ref, x_ref, mask_ref, wave_ref,
                 load_sem, small_sem, white, acc, core_in, tile_in,
                 energy_buf, edge_out, edge_in, core_send, core_recv, tile_send, tile_recv,
                 energy_send, energy_recv, edge_send, edge_recv):
    fibers, groups, block, bins, freqs = dims
    lag_count = groups * LAG_DEV
    fbits = fibers.bit_length() - 1
    gbits = groups.bit_length() - 1
    channels = fibers * block
    offsets = BAND + 1
    me = lax.axis_index("fiber")
    group = lax.axis_index("freq")

    def bit_of(value, k):
        return lax.rem(lax.div(value, 1 << k), 2)

    def partner(axis, k):
        place = me if axis == "fiber" else group
        return {axis: place + (1 - 2 * bit_of(place, k)) * (1 << k)}

    fiber_axes = [("fiber", k) for k in range(1, fbits)]
    freq_axes = [("freq", k) for k in range(gbits)]
    near_axes, far_axes = fiber_axes[:1], fiber_axes[1:]
    named = {"x": freq_axes, "y": near_axes, "z": far_axes}
    orders = [sum((named[n] for n in names), []) for names in PORTIONS]
    portions = list(range(2 * offsets))
    half = block // 2
    steps = len(freq_axes) + len(fiber_axes)

    def mine(axis):
        return bit_of(me if axis[0] == "fiber" else group, axis[1])

    def tile_place(relative):
        b = bit_of(me, CORE_BIT)
        lag = 0
        for axis, r in relative.items():
            own = mine(axis)
            value = r * own + (1 - r) * (1 - own)
            if axis[0] == "fiber":
                b = b + value * (1 << axis[1])
            else:
                lag = lag + value * (1 << axis[1])
        return b, lag

    def half_of(p):
        return pl.ds((p % 2) * half, half)

    def place_in(s, slot):
        return (1 << steps) - (1 << (steps - s)) + slot

    def tile_copy(p, s, slot, b, lag):
        axis = orders[p][s]
        place = place_in(s, slot)
        return pltpu.make_async_remote_copy(
            src_ref=acc.at[b, p // 2, lag, half_of(p)],
            dst_ref=tile_in.at[p, place],
            send_sem=tile_send.at[p, place],
            recv_sem=tile_recv.at[p, place],
            device_id=partner(*axis),
            device_id_type=MESH,
        )

    def slot_of(p, s, relative):
        slot = 0
        for axis in orders[p][s + 1:]:
            slot = slot * 2 + relative[axis]
        return slot

    rows = LOAD_ROWS
    chunks = 2 * bins // rows

    def load(i):
        at = pl.ds(pl.multiple_of(i * rows, rows), rows)
        return pltpu.make_async_copy(x_hbm.at[at], x_ref.at[at], load_sem.at[i])

    small = [
        pltpu.make_async_copy(source, target, small_sem.at[i])
        for i, (source, target) in enumerate(
            [(mask_hbm, mask_ref), (wave_hbm, wave_ref), (reach_hbm, reach_ref)]
        )
    ]
    for i in range(chunks):
        load(i).start()
    for copy in small:
        copy.start()

    barrier = pltpu.get_barrier_semaphore()
    hyper = [("fiber", k) for k in range(fbits)] + freq_axes
    for axis in hyper:
        pl.semaphore_signal(barrier, inc=1, device_id=partner(*axis), device_id_type=MESH)
    near = [d for o in range(1, offsets) for d in (o, -o)]

    def inside(d):
        return jnp.logical_and(me + d >= 0, me + d < fibers)

    for d in near:
        @pl.when(inside(d))
        def _():
            pl.semaphore_signal(barrier, inc=1, device_id={"fiber": me + d}, device_id_type=MESH)

    white[:, pl.ds(channels, BAND * block)] = jnp.zeros((2 * bins, BAND * block), jnp.bfloat16)

    def add_energy(i, total):
        load(i).wait()
        part = x_ref[pl.ds(pl.multiple_of(i * rows, rows), rows), :].astype(jnp.float32)
        return total + jnp.sum(part * part, axis=0, keepdims=True)

    energy = lax.fori_loop(0, chunks, add_energy, jnp.zeros((1, channels), jnp.float32))
    peers = len(hyper)
    for d in near:
        peers = peers + jnp.where(inside(d), 1, 0)
    pl.semaphore_wait(barrier, peers)

    for copy in small:
        copy.wait()
    for k in range(gbits):
        energy_buf[2 * k] = energy
        copy = pltpu.make_async_remote_copy(
            src_ref=energy_buf.at[2 * k],
            dst_ref=energy_buf.at[2 * k + 1],
            send_sem=energy_send.at[k],
            recv_sem=energy_recv.at[k],
            device_id=partner("freq", k),
            device_id_type=MESH,
        )
        copy.start()
        copy.wait()
        energy = energy + energy_buf[2 * k + 1]
    scale = mask_ref[...].astype(jnp.float32) / jnp.sqrt(energy * (1.0 / freqs) + 1e-06)

    def whiten(i, carry):
        at = pl.ds(pl.multiple_of(i * rows, rows), rows)
        white[at, pl.ds(0, channels)] = (x_ref[at, :].astype(jnp.float32) * scale).astype(jnp.bfloat16)
        return carry

    lax.fori_loop(0, chunks, whiten, 0)

    first = pl.multiple_of(group * bins, bins)

    def block_tiles(b):
        start = pl.multiple_of(b * block, block)
        turned = white[:, pl.ds(start, block)].astype(jnp.float32).T
        upper, lower = turned[:, :bins], turned[:, bins:]
        right = white[:, pl.ds(start, offsets * block)]
        for lag in range(lag_count):
            c = wave_ref[pl.ds(lag, 1), pl.ds(first, bins)]
            s = wave_ref[pl.ds(lag_count + lag, 1), pl.ds(first, bins)]
            rotated = jnp.concatenate([c * upper - s * lower, s * upper + c * lower], axis=1)
            high = rotated.astype(jnp.bfloat16)
            low = (rotated - high.astype(jnp.float32)).astype(jnp.bfloat16)
            both = jnp.dot(
                jnp.concatenate([high, low], axis=0), right, preferred_element_type=jnp.float32
            )
            both = both[:block] + both[block:]
            for d in range(offsets):
                acc[b, d, lag] = both[:, d * block:(d + 1) * block]

    halves = fibers // 2
    core = bit_of(me, CORE_BIT)
    order_bits = near_axes + far_axes

    def relatives(j):
        found = {}
        for i, axis in enumerate(order_bits):
            found[axis] = bit_of(j, len(order_bits) - 1 - i)
        return found

    def core_copy(j, b):
        return pltpu.make_async_remote_copy(
            src_ref=acc.at[b],
            dst_ref=core_in.at[j],
            send_sem=core_send.at[j],
            recv_sem=core_recv.at[j],
            device_id=partner("fiber", CORE_BIT),
            device_id_type=MESH,
        )

    def finish(j):
        relative = relatives(j)
        b, _ = tile_place(relative)
        core_copy(j, b).wait_recv()
        acc[b] = acc[b] + core_in[j]
        for p in portions:
            lead = orders[p][0]
            for choice in range(1 << gbits):
                full = dict(relative)
                for i, axis in enumerate(freq_axes):
                    full[axis] = (choice >> i) & 1
                if lead in freq_axes:
                    if full[lead] == 0:
                        tile_copy(p, 0, slot_of(p, 0, full), *tile_place(full)).start()
                else:
                    @pl.when(full[lead] == 0)
                    def _():
                        tile_copy(p, 0, slot_of(p, 0, full), *tile_place(full)).start()

    def two_blocks(j, carry):
        b, _ = tile_place(relatives(j))
        other = b + 1 - 2 * core
        block_tiles(other)
        core_copy(j, other).start()

        @pl.when(j > 0)
        def _():
            finish(j - 1)

        block_tiles(b)
        return carry

    lax.fori_loop(0, halves, two_blocks, 0)
    finish(halves - 1)

    def ready(p, s, relative):
        if s < 0:
            turn = 0
            for axis in order_bits:
                turn = 2 * turn + relative[axis]
            return turn * TURN
        axis = orders[p][s]
        sent = ready(p, s - 1, {**relative, axis: 0}) + HOP
        return max(sent, ready(p, s - 1, {**relative, axis: 1}))

    events = []
    for s in range(steps):
        for slot in range(1 << (steps - 1 - s)):
            for p in portions:
                rest = orders[p][s + 1:]
                relative = {axis: 1 for axis in orders[p][: s + 1]}
                for i, axis in enumerate(rest):
                    relative[axis] = (slot >> (len(rest) - 1 - i)) & 1
                events.append((ready(p, s, relative), s, len(events), p, slot, relative))
    for _, s, _, p, slot, relative in sorted(events, key=lambda event: event[:3]):
        rest = orders[p][s + 1:]
        b, lag = tile_place(relative)
        tile_copy(p, s, slot, b, lag).wait_recv()
        part = acc[b, p // 2, lag, half_of(p)]
        acc[b, p // 2, lag, half_of(p)] = part + tile_in[p, place_in(s, slot)]
        if rest and relative[rest[0]] == 0:
            tile_copy(p, s + 1, slot_of(p, s + 1, relative), b, lag).start()

    reach = reach_ref[me]

    def edge_copy(d):
        return pltpu.make_async_remote_copy(
            src_ref=edge_out.at[d - 1],
            dst_ref=edge_in.at[d - 1],
            send_sem=edge_send.at[d - 1],
            recv_sem=edge_recv.at[d - 1],
            device_id={"fiber": me + d},
            device_id_type=MESH,
        )

    for d in range(1, offsets):
        usable = jnp.where(jnp.logical_and(d <= reach, me + d < fibers), 1.0, 0.0)
        tile = acc[me, d, group] * usable
        out_ref[BAND + d] = tile
        edge_out[d - 1] = tile.T

        @pl.when(inside(d))
        def _():
            edge_copy(d).start()
    out_ref[BAND] = acc[me, 0, group]

    for d in range(1, offsets):
        out_ref[BAND - d] = jnp.zeros((block, block), jnp.float32)

        @pl.when(inside(-d))
        def _():
            edge_copy(d).wait_recv()
            out_ref[BAND - d] = edge_in[d - 1]

    for d in range(1, offsets):
        @pl.when(inside(d))
        def _():
            edge_copy(d).wait_send()

    def drain(j, carry):
        b, _ = tile_place(relatives(j))
        core_copy(j, b + 1 - 2 * core).wait_send()
        return carry

    lax.fori_loop(0, halves, drain, 0)
    for s in range(steps):
        for slot in range(1 << (steps - 1 - s)):
            for p in portions:
                tile_copy(p, s, slot, me, 0).wait_send()


def fused(spectra, valid_mask, pair_reach):
    groups, fibers = lax.axis_size("freq"), lax.axis_size("fiber")
    bins, channels = spectra.shape[1], spectra.shape[3]
    block = channels // fibers
    freqs = bins * groups
    lag_count = groups * LAG_DEV
    offsets = BAND + 1
    angle = (
        2.0 * np.pi / transform_length * lag_step
        * np.arange(lag_count)[:, None] * (first_bin + np.arange(freqs))[None, :]
    )
    wave = jnp.asarray(np.concatenate([np.cos(angle), np.sin(angle)]).astype(np.float32))
    steps = (groups.bit_length() - 1) + (fibers.bit_length() - 2)
    slots = (1 << steps) - 1
    tile = (block, block)
    vmem = pl.BlockSpec(memory_space=pltpu.VMEM)
    sem = pltpu.SemaphoreType.DMA
    result = pl.pallas_call(
        functools.partial(fused_kernel, (fibers, groups, block, bins, freqs)),
        out_shape=jax.ShapeDtypeStruct((2 * BAND + 1,) + tile, jnp.float32),
        in_specs=[pl.BlockSpec(memory_space=pl.ANY)] * 4,
        out_specs=vmem,
        scratch_shapes=[
            pltpu.SMEM(pair_reach.shape, jnp.int32),
            pltpu.VMEM((2 * bins, channels), jnp.bfloat16),
            pltpu.VMEM(valid_mask.shape, jnp.int32),
            pltpu.VMEM(wave.shape, jnp.float32),
            sem((2 * bins // LOAD_ROWS,)), sem((3,)),
            pltpu.VMEM((2 * bins, channels + BAND * block), jnp.bfloat16),
            pltpu.VMEM((fibers, offsets, lag_count) + tile, jnp.float32),
            pltpu.VMEM((fibers // 2, offsets, lag_count) + tile, jnp.float32),
            pltpu.VMEM((2 * offsets, slots, block // 2, block), jnp.float32),
            pltpu.VMEM((2 * (groups.bit_length() - 1), 1, channels), jnp.float32),
            pltpu.VMEM((BAND,) + tile, jnp.float32),
            pltpu.VMEM((BAND,) + tile, jnp.float32),
            sem((fibers // 2,)), sem((fibers // 2,)),
            sem((2 * offsets, slots)), sem((2 * offsets, slots)),
            sem((groups.bit_length() - 1,)), sem((groups.bit_length() - 1,)),
            sem((BAND,)), sem((BAND,)),
        ],
        compiler_params=pltpu.CompilerParams(
            collective_id=0, has_side_effects=True, vmem_limit_bytes=60 * 1024 * 1024
        ),
    )(pair_reach, spectra.reshape(2 * bins, channels), valid_mask, wave)
    return result[None, :, None]


def power_of_two(n):
    return n & (n - 1) == 0


def fits_on_chip(fibers, groups, spectra):
    block = spectra.shape[3] // fibers
    partial_bytes = 4 * fibers * (BAND + 1) * groups * LAG_DEV * block * block
    return (
        power_of_two(fibers) and power_of_two(groups) and fibers >= 8 and groups >= 2
        and block % 128 == 0 and spectra.shape[1] % 128 == 0 and partial_bytes <= 1 << 23
    )


def shards(spectra, valid_mask, pair_reach):
    if fits_on_chip(lax.axis_size("fiber"), lax.axis_size("freq"), spectra):
        return fused(spectra, valid_mask, pair_reach)
    return spread(spectra, valid_mask, pair_reach)


def solution(mesh):
    return jax.shard_map(
        shards,
        mesh=mesh,
        in_specs=(P(None, "freq", "fiber", None), P("fiber", None), P()),
        out_specs=P("fiber", None, "freq", None, None),
        check_vma=False,
    )
```
